32 devices in a mesh: gx: 4 (over y, x), gy: 8 (over z, core).
Axes of the slice: x: 2, y: 2, z: 4, core: 2. Of those that a mesh axis runs over, the one named last changes fastest.
Arguments:
- atom_cell: int32 [4, 8, 4096], P('gx', 'gy'), may hold values from 0 to 49151
- atom_frac: float32 [3, 4, 8, 4096], P(None, 'gx', 'gy'), may hold values from 0 to 1
- atom_charge: float32 [4, 8, 4096], P('gx', 'gy'), may hold values from -6 to 6
- atom_count: int32 [4, 8], P('gx', 'gy'), may hold values from 1024 to 4096, as said below
- fine_kernel: float32 [9, 9, 9], replicated, may hold values from -1.8 to 1.8
- middle_kernel: float32 [9, 9, 9], replicated, may hold values from -0.9 to 0.9
- coarse_kernel: float32 [9, 9, 9], replicated, may hold values from -0.36 to 0.36
Outputs:
- potential: float32 [64, 192, 128], P('gx', 'gy')
- forces: float32 [3, 4, 8, 4096], P(None, 'gx', 'gy')
The draws below stay inside these ranges and needn't reach their ends.
Inputs may be any that keep to these rules, and one draw needn't show every extreme that they name: `atom_count`: slots at or past a block's count hold no atom. At least one block is full in every draw; about a quarter of the blocks are nearly full and the rest hold a quarter to a half of 4096.
All inputs are finite; a program needn't handle non-finite values.
Results may differ from the reference program's by a relative error of at most 0.0003.
Values sent between devices are 32-bit elements; how exact they have to be, the bound alone decides.
A program may use at most 128 MiB of HBM per device.

```python
import jax
import jax.numpy as jnp
from jax import lax

CX = 16
CY = 24
NZ = 128
ATOMS_DEV = 4096
KERNEL = 9
NX = 64
NY = 192
N_GX = 4
N_GY = 8


def draw_atom_count(key, part):
    key_low = jax.random.fold_in(key, 11)
    key_high = jax.random.fold_in(key, 12)
    key_pick = jax.random.fold_in(key, 13)
    key_full = jax.random.fold_in(key, 14)
    light = jax.random.randint(key_low, (N_GX, N_GY), ATOMS_DEV // 4, ATOMS_DEV // 2 + 1)
    heavy = ATOMS_DEV - jax.random.randint(key_high, (N_GX, N_GY), 0, ATOMS_DEV // 8)
    chosen = jax.random.randint(key_pick, (N_GX, N_GY), 0, 4) == 0
    counts = jnp.where(chosen, heavy, light).reshape(-1)
    fullest = jax.random.randint(key_full, (), 0, N_GX * N_GY)
    counts = jnp.where(jnp.arange(N_GX * N_GY) == fullest, ATOMS_DEV, counts)
    return counts.reshape(N_GX, N_GY).astype(jnp.int32)


def set_ends(entries, rng, least, high):
    spot = [jax.random.randint(jax.random.fold_in(rng, axis), (), 0, length) for axis, length in enumerate(entries.shape)]
    main_axis = entries.shape.index(max(entries.shape))
    next_to = spot[:main_axis] + [(spot[main_axis] + 1) % entries.shape[main_axis]] + spot[main_axis + 1:]
    return entries.at[tuple(spot)].set(least).at[tuple(next_to)].set(high)


def block_scale(own_key, extent, shards, least, high):
    gain, own = 1.0, jax.random.fold_in(own_key, 6)
    for axis_at, blocks in shards:
        steps = jnp.exp(jax.random.uniform(jax.random.fold_in(own, axis_at), (blocks,), jnp.float32, least / len(shards), high / len(shards)))
        gain = gain * jnp.repeat(steps, extent[axis_at] // blocks).reshape([-1 if axis == axis_at else 1 for axis in range(len(extent))])
    return gain


def normal_values(stream_key, shape, spread, reach, split=(), held_as=jnp.bfloat16):
    result = jax.random.normal(stream_key, shape, jnp.float32) * spread
    if len(split) > 0:
        result = block_scale(stream_key, shape, split, -0.22, 0.18) * result
    return jnp.clip(result, min=-reach, max=reach).astype(held_as)


def setup_inputs(seed: int = 0) -> dict:
    keys = jax.random.split(jax.random.key(seed), 8)
    atom_cell = set_ends(jax.random.randint(keys[0], (N_GX, N_GY, ATOMS_DEV), 0, CX * CY * NZ), jax.random.fold_in(keys[0], 1), 0, (CX * CY * NZ) - 1).astype(jnp.int32)
    atom_frac = jnp.clip(1.0 * jax.random.uniform(keys[1], (3, N_GX, N_GY, ATOMS_DEV), jnp.float32) ** block_scale(keys[1], (3, N_GX, N_GY, ATOMS_DEV), ((1, 4), (2, 8)), -0.2, 0.2), 0.0, 1.0)
    atom_charge = normal_values(keys[2], (N_GX, N_GY, ATOMS_DEV), 1.0, 6.0, ((0, 4), (1, 8)), jnp.float32)
    atom_count = draw_atom_count(jax.random.fold_in(keys[7], 71), 0)
    fine_kernel = normal_values(keys[4], (KERNEL, KERNEL, KERNEL), 0.3, 1.8, (), jnp.float32)
    middle_kernel = normal_values(keys[5], (KERNEL, KERNEL, KERNEL), 0.15, 0.9, (), jnp.float32)
    coarse_kernel = normal_values(keys[6], (KERNEL, KERNEL, KERNEL), 0.06, 0.36, (), jnp.float32)
    return dict(atom_cell=atom_cell, atom_frac=atom_frac, atom_charge=atom_charge, atom_count=atom_count, fine_kernel=fine_kernel, middle_kernel=middle_kernel, coarse_kernel=coarse_kernel)


def kernel_grid(kernel, grid_shape):
    half_width = KERNEL // 2
    offsets = jnp.arange(KERNEL, dtype=jnp.int32)
    place_x = jnp.mod(half_width - offsets, grid_shape[0])
    place_y = jnp.mod(half_width - offsets, grid_shape[1])
    place_z = jnp.mod(half_width - offsets, grid_shape[2])
    empty = jnp.zeros(grid_shape, jnp.float32)
    return empty.at[place_x[:, None, None], place_y[None, :, None], place_z[None, None, :]].add(kernel)


def convolve_whole(grid_in, kernel):
    spectrum = jnp.fft.rfftn(grid_in) * jnp.fft.rfftn(kernel_grid(kernel, grid_in.shape).astype(grid_in.dtype))
    return jnp.fft.irfftn(spectrum, s=grid_in.shape).astype(grid_in.dtype)


def restrict_whole(grid_in):
    for dimension in range(3):
        grid_in = 0.5 * jnp.roll(grid_in, 1, dimension) + grid_in + 0.5 * jnp.roll(grid_in, -1, dimension)
        grid_in = lax.slice_in_dim(grid_in, 0, grid_in.shape[dimension], 2, dimension)
    return grid_in


def prolong_whole(grid_in):
    for dimension in range(3):
        paired = jnp.stack([grid_in, 0.5 * (grid_in + jnp.roll(grid_in, -1, dimension))], axis=dimension + 1)
        new_shape = list(grid_in.shape)
        new_shape[dimension] = 2 * new_shape[dimension]
        grid_in = paired.reshape(new_shape)
    return grid_in


def reference(atom_cell, atom_frac, atom_charge, atom_count, fine_kernel, middle_kernel, coarse_kernel):
    block_x = jnp.arange(N_GX, dtype=jnp.int32)[:, None, None]
    block_y = jnp.arange(N_GY, dtype=jnp.int32)[None, :, None]
    base_x = block_x * CX + atom_cell // (CY * NZ)
    base_y = block_y * CY + (atom_cell // NZ) % CY
    base_z = atom_cell % NZ
    slot_index = jnp.arange(ATOMS_DEV, dtype=jnp.int32)[None, None, :]
    is_live = slot_index < atom_count[:, :, None]
    live_charge = jnp.where(is_live, atom_charge, 0.0)
    corner_ids = []
    weights = []
    slopes = []
    for corner in range(8):
        raised = [(corner >> 2) & 1, (corner >> 1) & 1, corner & 1]
        factors = [atom_frac[dimension] if raised[dimension] else 1.0 - atom_frac[dimension] for dimension in range(3)]
        sign_list = [1.0 if raised[dimension] else -1.0 for dimension in range(3)]
        flat_index = ((base_x + raised[0]) % NX * NY + (base_y + raised[1]) % NY) * NZ + (base_z + raised[2]) % NZ
        corner_ids.append(flat_index.astype(jnp.int32))
        weights.append(factors[0] * factors[1] * factors[2])
        slopes.append(jnp.stack([sign_list[0] * factors[1] * factors[2], factors[0] * sign_list[1] * factors[2], factors[0] * factors[1] * sign_list[2]]))
    corner_ids = jnp.stack(corner_ids)
    weights = jnp.stack(weights)
    spread_values = weights * live_charge[None]
    fine_charge = jax.ops.segment_sum(spread_values.reshape(-1), corner_ids.reshape(-1), num_segments=NX * NY * NZ).reshape(NX, NY, NZ)
    middle_charge = restrict_whole(fine_charge)
    coarse_charge = restrict_whole(middle_charge)
    coarse_potential = convolve_whole(coarse_charge, coarse_kernel)
    middle_potential = convolve_whole(middle_charge, middle_kernel) + prolong_whole(coarse_potential)
    potential = convolve_whole(fine_charge, fine_kernel) + prolong_whole(middle_potential)
    flat_potential = potential.reshape(-1)
    running = jnp.zeros((3, N_GX, N_GY, ATOMS_DEV), potential.dtype)
    for corner in range(8):
        running = running + slopes[corner] * flat_potential[corner_ids[corner]][None]
    forces = -live_charge[None] * running
    return potential, forces
```

```python
import jax
import jax.numpy as jnp
from jax import lax
from jax.experimental import pallas as pl
from jax.experimental.pallas import tpu as pltpu
from jax.sharding import PartitionSpec as P

CX = 16
CY = 24
NZ = 128
KERNEL = 9
HALF = KERNEL // 2
LANES = 128
CHUNK = 512
MESH = pl.DeviceIdType.MESH

BX = (CX, CX // 2, CX // 4)
BY = (CY, CY // 2, CY // 4)
RY = tuple(-(-(size + 1) // 8) * 8 for size in BY)
ZS = (NZ, NZ // 2, NZ // 4)
COARSE_LANE = ZS[1]


def split(value):
    high = value.astype(jnp.bfloat16)
    return high, (value - high.astype(jnp.float32)).astype(jnp.bfloat16)


def matmul(a, b):
    return jnp.dot(a, b, preferred_element_type=jnp.float32)


def matmul_nt(a, b):
    return lax.dot_general(a, b, (((1,), (1,)), ((), ())), preferred_element_type=jnp.float32)


def exact(a, b):
    return jnp.dot(a, b, preferred_element_type=jnp.float32, precision=lax.Precision.HIGHEST)


def hat(distance):
    return jnp.maximum(1.0 - jnp.abs(distance), 0.0)


def ring_hat(distance, period):
    distance = jnp.abs(distance)
    return jnp.maximum(1.0 - jnp.minimum(distance, period - distance), 0.0)


def rows_iota(rows, columns):
    return lax.broadcasted_iota(jnp.int32, (rows, columns), 0)


def bases(cell):
    return cell // (CY * NZ), (cell // NZ) % CY, cell % NZ


def spread_kernel(count_ref, cell_ref, frac_ref, charge_ref, fine_ref, strip_ref, middle_ref, coarse_ref):
    slots = cell_ref.shape[1]
    fine = jnp.zeros((fine_ref.shape[0] * RY[0], LANES), jnp.float32)
    rest = jnp.zeros(((BX[1] + 1) * RY[1] + (BX[2] + 1) * RY[2], LANES), jnp.float32)
    for start in range(0, slots, CHUNK):
        part = slice(start, start + CHUNK)
        base = bases(cell_ref[:, part])
        place = [base[k].astype(jnp.float32) + frac_ref[k : k + 1, part] for k in range(3)]
        slot = start + lax.broadcasted_iota(jnp.int32, (1, CHUNK), 1)
        charge = jnp.where(slot < count_ref[0, 0], charge_ref[:, part], 0.0)
        tops = []
        for level in range(3):
            scale = 0.5**level
            row_x = rows_iota(-(-(BX[level] + 1) // 8) * 8, CHUNK).astype(jnp.float32)
            row_y = rows_iota(RY[level], CHUNK).astype(jnp.float32)
            weight_x = hat(place[0] * scale - row_x) * charge
            weight_y = hat(place[1] * scale - row_y)
            tops.append(
                jnp.concatenate([weight_x[x : x + 1] * weight_y for x in range(BX[level] + 1)], axis=0)
            )
        z_fine = ring_hat(place[2] - rows_iota(NZ, CHUNK).astype(jnp.float32), float(NZ))
        z_middle = ring_hat(place[2] * 0.5 - rows_iota(ZS[1], CHUNK).astype(jnp.float32), float(ZS[1]))
        z_coarse = ring_hat(place[2] * 0.25 - rows_iota(ZS[2], CHUNK).astype(jnp.float32), float(ZS[2]))
        z_rest = jnp.concatenate([z_middle, z_coarse, jnp.zeros_like(z_coarse)], axis=0)
        for which, top, z_side in ((0, tops[0], z_fine), (1, jnp.concatenate(tops[1:], axis=0), z_rest)):
            top_high, top_low = split(top)
            z_high, z_low = split(z_side)
            both = matmul_nt(top_high, jnp.concatenate([z_high, z_low], axis=0))
            term = both[:, :LANES] + both[:, LANES:] + matmul_nt(top_low, z_high)
            if which == 0:
                fine = fine + term
            else:
                rest = rest + term
    fine = fine.reshape(BX[0] + 1, RY[0], LANES)
    fine_ref[...] = fine
    strip_ref[...] = fine[:, BY[0] - HALF : BY[0] - HALF + 8, :]
    rows = (BX[1] + 1) * RY[1]
    middle_ref[...] = rest[:rows].reshape(BX[1] + 1, RY[1], LANES)
    coarse_ref[...] = rest[rows:].reshape(BX[2] + 1, RY[2], LANES)


def transfers():
    plans = []
    for level in range(3):
        far = 2 if level == 2 else 1
        for dx in range(-far, far + 1):
            for dy in (-1, 0, 1):
                if dx == 0 and dy == 0:
                    continue
                low_x = max(0, dx * BX[level] - HALF)
                high_x = min(BX[level] + 1, dx * BX[level] + BX[level] + HALF + 1)
                source = level
                low_y, size_y = 0, RY[level]
                shift = 0
                if level == 0 and dy == 1:
                    source, low_y, size_y, shift = 3, 0, 8, BY[0] - HALF
                elif level < 2 and dy == -1:
                    size_y = 8
                elif level == 1 and dy == 1:
                    low_y, size_y = 8, 8
                at_x = low_x - dx * BX[level]
                at_y = low_y + shift - dy * BY[level]
                plans.append((level, dx, dy, source, low_x, high_x - low_x, low_y, size_y, at_x, at_y))
    return plans


PLANS = transfers()


def exchange_kernel(sizes, *refs):
    sources = refs[:4]
    targets = refs[4 : 4 + len(PLANS)]
    send_sem, recv_sem = refs[4 + len(PLANS) :]
    me = (lax.axis_index("gx"), lax.axis_index("gy"))

    def device(dx, dy):
        return (lax.rem(me[0] + dx + sizes[0], sizes[0]), lax.rem(me[1] + dy + sizes[1], sizes[1]))

    barrier = pltpu.get_barrier_semaphore()
    around = sorted({(plan[1], plan[2]) for plan in PLANS})
    for dx, dy in around:
        pl.semaphore_signal(barrier, inc=1, device_id=device(dx, dy), device_id_type=MESH)
    pl.semaphore_wait(barrier, len(around))
    copies = []
    for index, (_, dx, dy, source, low_x, size_x, low_y, size_y, _, _) in enumerate(PLANS):
        copies.append(
            pltpu.make_async_remote_copy(
                src_ref=sources[source].at[pl.ds(low_x, size_x), pl.ds(low_y, size_y)],
                dst_ref=targets[index],
                send_sem=send_sem.at[index],
                recv_sem=recv_sem.at[index],
                device_id=device(dx, dy),
                device_id_type=MESH,
            )
        )
    for copy in copies:
        copy.start()
    for copy in copies:
        copy.wait()


def build_tables(kernel_ref, high_ref, low_ref, z_size, z_from_lane):
    packed = LANES // z_size
    blocks = -(-KERNEL // packed)
    row = rows_iota(8, LANES)
    lane = lax.broadcasted_iota(jnp.int32, (8, LANES), 1)
    tap = lax.rem(row - lane + HALF + 2 * LANES, z_size)

    def step(shift_x, carry):
        for block in range(blocks):
            for inner in range(packed):
                shift_y = block * packed + inner
                top = jnp.zeros((8, LANES), jnp.float32)
                if shift_y < KERNEL:
                    for c in range(KERNEL):
                        value = kernel_ref[shift_x, shift_y * KERNEL + c]
                        top = jnp.where(tap == c, value, top)
                pieces = [top]
                for piece in range(1, z_size // 8):
                    pieces.append(pltpu.roll(top, 8 * piece, 1))
                table_high, table_low = split(jnp.concatenate(pieces, axis=0))
                place = slice(block * LANES + inner * z_size, block * LANES + (inner + 1) * z_size)
                high_ref[shift_x, place, :] = table_high
                low_ref[shift_x, place, :] = table_low
        return carry

    lax.fori_loop(0, KERNEL, step, 0)


def pack_taps(padded, z_size, rows):
    packed = LANES // z_size
    group = lax.broadcasted_iota(jnp.int32, (1, 1, LANES), 2) // z_size
    blocks = []
    for block in range(-(-KERNEL // packed)):
        value = padded[:, block * packed : block * packed + rows, :]
        for inner in range(1, packed):
            first = block * packed + inner
            if first < KERNEL:
                value = jnp.where(group == inner, padded[:, first : first + rows, :], value)
        blocks.append(value)
    return blocks


def potential_kernel(*refs):
    kernels = refs[:3]
    own = refs[3:6]
    arrived = refs[6 : 6 + len(PLANS)]
    out_ref = refs[6 + len(PLANS)]
    scratch = refs[7 + len(PLANS) :]
    padded_refs, table_refs, joined_refs = scratch[:3], scratch[3:9], scratch[9:15]
    results = []
    for level in (2, 1, 0):
        x_out, rows = BX[level] + 1, RY[level]
        padded = padded_refs[level]
        padded[...] = jnp.zeros_like(padded)
        padded[HALF : HALF + x_out, 8 : 8 + rows, :] = own[level][...]
        for index, plan in enumerate(PLANS):
            if plan[0] == level:
                size_x, size_y, at_x, at_y = plan[5], plan[7], plan[8], plan[9]
                xs = slice(HALF + at_x, HALF + at_x + size_x)
                ys = slice(8 + at_y, 8 + at_y + size_y)
                padded[xs, ys, :] = padded[xs, ys, :] + arrived[index][...]
        high_table, low_table = table_refs[2 * level], table_refs[2 * level + 1]
        build_tables(kernels[level], high_table, low_table, ZS[level], 0)
        joined_high, joined_low = joined_refs[2 * level], joined_refs[2 * level + 1]
        copied = LANES // ZS[level]
        whole = padded[:, HALF : HALF + rows + KERNEL - 1 + copied, :]
        if level > 0:
            first = 0 if level == 1 else COARSE_LANE
            lanes = lax.broadcasted_iota(jnp.int32, (1, 1, LANES), 2)
            whole = jnp.where((lanes >= first) & (lanes < first + ZS[level]), whole, 0.0)
            shape = whole.shape
            flat = whole.reshape(shape[0] * shape[1], LANES)
            source = rows_iota(LANES, LANES)
            target = lax.broadcasted_iota(jnp.int32, (LANES, LANES), 1)
            repeat = (lax.rem(target, ZS[level]) + first == source).astype(jnp.float32)
            whole = exact(flat, repeat).reshape(shape)
        for block, value in enumerate(pack_taps(whole, ZS[level], rows)):
            value_high, value_low = split(value)
            joined_high[:, :, block * LANES : (block + 1) * LANES] = value_high
            joined_low[:, :, block * LANES : (block + 1) * LANES] = value_low
        total = jnp.zeros((x_out * rows, LANES), jnp.float32)
        for shift_x in range(KERNEL):
            left_high = joined_high[shift_x : shift_x + x_out].reshape(x_out * rows, -1)
            left_low = joined_low[shift_x : shift_x + x_out].reshape(x_out * rows, -1)
            total = total + matmul(left_high, high_table[shift_x])
            total = total + matmul(left_low, high_table[shift_x])
            total = total + matmul(left_high, low_table[shift_x])
        if level < 2:
            below = results[-1]
            z_low = rows_iota(LANES, LANES)
            lane = lax.broadcasted_iota(jnp.int32, (LANES, LANES), 1)
            lane = lax.rem(lane, ZS[level])
            z_weight = ring_hat(lane.astype(jnp.float32) * 0.5 - z_low.astype(jnp.float32), float(ZS[level + 1]))
            z_weight = jnp.where(z_low < ZS[level + 1], z_weight, 0.0)
            below = exact(below, z_weight)
            rows_below = RY[level + 1]
            count_below = (BX[level + 1] + 1) * rows_below
            fine_row = rows_iota(x_out * rows, count_below)
            low_row = lax.broadcasted_iota(jnp.int32, (x_out * rows, count_below), 1)
            weight = hat((fine_row // rows).astype(jnp.float32) * 0.5 - (low_row // rows_below).astype(jnp.float32))
            weight = weight * hat(
                lax.rem(fine_row, rows).astype(jnp.float32) * 0.5 - lax.rem(low_row, rows_below).astype(jnp.float32)
            )
            total = total + exact(weight, below)
        results.append(total)
    out_ref[...] = results[-1].reshape(BX[0] + 1, RY[0], LANES)


def force_kernel(count_ref, cell_ref, frac_ref, charge_ref, potential_ref, forces_ref):
    slots = cell_ref.shape[1]
    rows = RY[0]
    grid_in = potential_ref[...].reshape((BX[0] + 1) * rows, LANES)
    left = jnp.concatenate(split(grid_in), axis=1)
    for start in range(0, slots, CHUNK):
        part = slice(start, start + CHUNK)
        base_x, base_y, base_z = bases(cell_ref[:, part])
        frac = [frac_ref[k : k + 1, part] for k in range(3)]
        slot = start + lax.broadcasted_iota(jnp.int32, (1, CHUNK), 1)
        charge = jnp.where(slot < count_ref[0, 0], charge_ref[:, part], 0.0)
        row_z = rows_iota(NZ, CHUNK)
        pick_low = jnp.where(row_z == base_z, 1.0, 0.0).astype(jnp.bfloat16)
        pick_high = jnp.where(row_z == lax.rem(base_z + 1, NZ), 1.0, 0.0).astype(jnp.bfloat16)
        low = matmul(left, jnp.concatenate([pick_low, pick_low], axis=0))
        high = matmul(left, jnp.concatenate([pick_high, pick_high], axis=0))
        slope = high - low
        level = low + frac[2] * slope
        row_x = rows_iota(-(-(BX[0] + 1) // 8) * 8, CHUNK)
        row_y = rows_iota(rows, CHUNK)

        def sides(row, base, f):
            lower, upper = row == base, row == base + 1
            weight = jnp.where(lower, 1.0 - f, jnp.where(upper, f, 0.0))
            sign = jnp.where(lower, -1.0, jnp.where(upper, 1.0, 0.0))
            return weight, sign

        weight_x, sign_x = sides(row_x, base_x, frac[0])
        weight_y, sign_y = sides(row_y, base_y, frac[1])
        in_x = jnp.zeros((rows, CHUNK), jnp.float32)
        across_x = jnp.zeros((rows, CHUNK), jnp.float32)
        in_z = jnp.zeros((rows, CHUNK), jnp.float32)
        for x in range(BX[0] + 1):
            piece = level[x * rows : (x + 1) * rows]
            in_x = in_x + weight_x[x : x + 1] * piece
            across_x = across_x + sign_x[x : x + 1] * piece
            in_z = in_z + weight_x[x : x + 1] * slope[x * rows : (x + 1) * rows]
        forces_ref[0:1, part] = -charge * jnp.sum(weight_y * across_x, axis=0, keepdims=True)
        forces_ref[1:2, part] = -charge * jnp.sum(sign_y * in_x, axis=0, keepdims=True)
        forces_ref[2:3, part] = -charge * jnp.sum(weight_y * in_z, axis=0, keepdims=True)


VMEM = pl.BlockSpec(memory_space=pltpu.VMEM)
SMEM = pl.BlockSpec(memory_space=pltpu.SMEM)


def grid_shape(level):
    return jax.ShapeDtypeStruct((BX[level] + 1, RY[level], LANES), jnp.float32)


def solution(mesh):
    sizes = (mesh.shape["gx"], mesh.shape["gy"])

    def per_device(atom_cell, atom_frac, atom_charge, atom_count, fine_kernel, middle_kernel, coarse_kernel):
        slots = atom_cell.shape[-1]
        cell = atom_cell.reshape(1, slots)
        frac = atom_frac.reshape(3, slots)
        charge = atom_charge.reshape(1, slots)
        raw = pl.pallas_call(
            spread_kernel,
            out_shape=(
                grid_shape(0),
                jax.ShapeDtypeStruct((BX[0] + 1, 8, LANES), jnp.float32),
                grid_shape(1),
                grid_shape(2),
            ),
            in_specs=[SMEM, VMEM, VMEM, VMEM],
            out_specs=(VMEM,) * 4,
            name="spread",
        )(atom_count, cell, frac, charge)
        fine, strip, middle, coarse = raw
        arrived = pl.pallas_call(
            lambda *refs: exchange_kernel(sizes, *refs),
            out_shape=tuple(jax.ShapeDtypeStruct((plan[5], plan[7], LANES), jnp.float32) for plan in PLANS),
            in_specs=[VMEM] * 4,
            out_specs=(VMEM,) * len(PLANS),
            scratch_shapes=[
                pltpu.SemaphoreType.DMA((len(PLANS),)),
                pltpu.SemaphoreType.DMA((len(PLANS),)),
            ],
            compiler_params=pltpu.CompilerParams(collective_id=0, has_side_effects=True),
            name="exchange",
        )(fine, middle, coarse, strip)
        kernels = [k.reshape(KERNEL, KERNEL * KERNEL) for k in (fine_kernel, middle_kernel, coarse_kernel)]
        padded_shapes, table_shapes, joined_shapes = [], [], []
        for level in range(3):
            packed = LANES // ZS[level]
            depth = -(-KERNEL // packed) * LANES
            x_in = BX[level] + KERNEL
            padded_shapes.append(pltpu.VMEM((x_in, RY[level] + 24, LANES), jnp.float32))
            table_shapes += [pltpu.VMEM((KERNEL, depth, LANES), jnp.bfloat16)] * 2
            joined_shapes += [pltpu.VMEM((x_in, RY[level], depth), jnp.bfloat16)] * 2
        extended = pl.pallas_call(
            potential_kernel,
            out_shape=grid_shape(0),
            in_specs=[SMEM] * 3 + [VMEM] * (3 + len(PLANS)),
            out_specs=VMEM,
            scratch_shapes=padded_shapes + table_shapes + joined_shapes,
            name="potential",
        )(*kernels, fine, middle, coarse, *arrived)
        forces = pl.pallas_call(
            force_kernel,
            out_shape=jax.ShapeDtypeStruct((3, slots), jnp.float32),
            in_specs=[SMEM, VMEM, VMEM, VMEM, VMEM],
            out_specs=VMEM,
            name="forces",
        )(atom_count, cell, frac, charge, extended)
        return extended[:CX, :CY], forces.reshape(3, 1, 1, slots)

    return jax.shard_map(
        per_device,
        mesh=mesh,
        in_specs=(
            P("gx", "gy", None),
            P(None, "gx", "gy", None),
            P("gx", "gy", None),
            P("gx", "gy"),
            P(),
            P(),
            P(),
        ),
        out_specs=(P("gx", "gy", None), P(None, "gx", "gy", None)),
        check_vma=False,
    )
```

```python
import jax
import jax.numpy as jnp
from jax import lax
from jax.experimental import pallas as pl
from jax.experimental.pallas import tpu as pltpu
from jax.sharding import PartitionSpec as P

CX = 16
CY = 24
NZ = 128
KERNEL = 9
HALF = KERNEL // 2
LANES = 128
CHUNK = 512
MESH = pl.DeviceIdType.MESH

BX = (CX, CX // 2, CX // 4)
BY = (CY, CY // 2, CY // 4)
RY = tuple(-(-(size + 1) // 8) * 8 for size in BY)
ZS = (NZ, NZ // 2, NZ // 4)
COARSE_LANE = ZS[1]


def split(value):
    high = value.astype(jnp.bfloat16)
    return high, (value - high.astype(jnp.float32)).astype(jnp.bfloat16)


def matmul(a, b):
    return jnp.dot(a, b, preferred_element_type=jnp.float32)


def matmul_nt(a, b):
    return lax.dot_general(a, b, (((1,), (1,)), ((), ())), preferred_element_type=jnp.float32)


def exact(a, b):
    return jnp.dot(a, b, preferred_element_type=jnp.float32, precision=lax.Precision.HIGHEST)


def hat(distance):
    return jnp.maximum(1.0 - jnp.abs(distance), 0.0)


def ring_hat(distance, period):
    distance = jnp.abs(distance)
    return jnp.maximum(1.0 - jnp.minimum(distance, period - distance), 0.0)


def rows_iota(rows, columns):
    return lax.broadcasted_iota(jnp.int32, (rows, columns), 0)


def bases(cell):
    return cell // (CY * NZ), (cell // NZ) % CY, cell % NZ


def spread_kernel(count_ref, cell_ref, frac_ref, charge_ref, fine_ref, strip_ref, middle_ref, coarse_ref):
    slots = cell_ref.shape[-1]
    fine = jnp.zeros((fine_ref.shape[0] * RY[0], LANES), jnp.float32)
    rest = jnp.zeros(((BX[1] + 1) * RY[1] + (BX[2] + 1) * RY[2], LANES), jnp.float32)
    for start in range(0, slots, CHUNK):
        part = slice(start, start + CHUNK)
        base = bases(cell_ref[0, :, part])
        place = [base[k].astype(jnp.float32) + frac_ref[k, 0, :, part] for k in range(3)]
        slot = start + lax.broadcasted_iota(jnp.int32, (1, CHUNK), 1)
        charge = jnp.where(slot < count_ref[0, 0], charge_ref[0, :, part], 0.0)
        tops = []
        for level in range(3):
            scale = 0.5**level
            row_x = rows_iota(-(-(BX[level] + 1) // 8) * 8, CHUNK).astype(jnp.float32)
            row_y = rows_iota(RY[level], CHUNK).astype(jnp.float32)
            weight_x = hat(place[0] * scale - row_x) * charge
            weight_y = hat(place[1] * scale - row_y)
            tops.append(
                jnp.concatenate([weight_x[x : x + 1] * weight_y for x in range(BX[level] + 1)], axis=0)
            )
        z_fine = ring_hat(place[2] - rows_iota(NZ, CHUNK).astype(jnp.float32), float(NZ))
        z_middle = ring_hat(place[2] * 0.5 - rows_iota(ZS[1], CHUNK).astype(jnp.float32), float(ZS[1]))
        z_coarse = ring_hat(place[2] * 0.25 - rows_iota(ZS[2], CHUNK).astype(jnp.float32), float(ZS[2]))
        z_rest = jnp.concatenate([z_middle, z_coarse, jnp.zeros_like(z_coarse)], axis=0)
        for which, top, z_side in ((0, tops[0], z_fine), (1, jnp.concatenate(tops[1:], axis=0), z_rest)):
            top_high, top_low = split(top)
            z_high, z_low = split(z_side)
            both = matmul_nt(top_high, jnp.concatenate([z_high, z_low], axis=0))
            term = both[:, :LANES] + both[:, LANES:] + matmul_nt(top_low, z_high)
            if which == 0:
                fine = fine + term
            else:
                rest = rest + term
    fine = fine.reshape(BX[0] + 1, RY[0], LANES)
    fine_ref[...] = fine
    strip_ref[...] = fine[:, BY[0] - HALF : BY[0] - HALF + 8, :]
    rows = (BX[1] + 1) * RY[1]
    middle_ref[...] = rest[:rows].reshape(BX[1] + 1, RY[1], LANES)
    coarse_ref[...] = rest[rows:].reshape(BX[2] + 1, RY[2], LANES)


def transfers():
    plans = []
    for level in range(3):
        far = 2 if level == 2 else 1
        for dx in range(-far, far + 1):
            for dy in (-1, 0, 1):
                if dx == 0 and dy == 0:
                    continue
                low_x = max(0, dx * BX[level] - HALF)
                high_x = min(BX[level] + 1, dx * BX[level] + BX[level] + HALF + 1)
                source = level
                low_y, size_y = 0, RY[level]
                shift = 0
                if level == 0 and dy == 1:
                    source, low_y, size_y, shift = 3, 0, 8, BY[0] - HALF
                elif level < 2 and dy == -1:
                    size_y = 8
                elif level == 1 and dy == 1:
                    low_y, size_y = 8, 8
                at_x = low_x - dx * BX[level]
                at_y = low_y + shift - dy * BY[level]
                plans.append((level, dx, dy, source, low_x, high_x - low_x, low_y, size_y, at_x, at_y))
    return plans


PLANS = transfers()


def halo_copies(sizes, sources, targets, send_sem, recv_sem):
    me = (lax.axis_index("gx"), lax.axis_index("gy"))

    def device(dx, dy):
        return (lax.rem(me[0] + dx + sizes[0], sizes[0]), lax.rem(me[1] + dy + sizes[1], sizes[1]))

    barrier = pltpu.get_barrier_semaphore()
    around = sorted({(plan[1], plan[2]) for plan in PLANS})
    for dx, dy in around:
        pl.semaphore_signal(barrier, inc=1, device_id=device(dx, dy), device_id_type=MESH)
    pl.semaphore_wait(barrier, len(around))
    copies = []
    for index, (_, dx, dy, source, low_x, size_x, low_y, size_y, _, _) in enumerate(PLANS):
        copies.append(
            pltpu.make_async_remote_copy(
                src_ref=sources[source].at[pl.ds(low_x, size_x), pl.ds(low_y, size_y)],
                dst_ref=targets[index],
                send_sem=send_sem.at[index],
                recv_sem=recv_sem.at[index],
                device_id=device(dx, dy),
                device_id_type=MESH,
            )
        )
    return copies


def build_tables(kernel_ref, high_ref, low_ref, z_size, pair):
    packed = LANES // z_size
    blocks = -(-KERNEL // packed)
    row = rows_iota(8, LANES)
    lane = lax.broadcasted_iota(jnp.int32, (8, LANES), 1)
    tap = lax.rem(row - lane + HALF + 2 * LANES, z_size)

    def step(shift_x, carry):
        for block in range(blocks):
            for inner in range(packed):
                shift_y = block * packed + inner
                top = jnp.zeros((8, LANES), jnp.float32)
                if shift_y < KERNEL:
                    for c in range(KERNEL):
                        value = kernel_ref[shift_x, shift_y, c]
                        top = jnp.where(tap == c, value, top)
                pieces = [top]
                for piece in range(1, z_size // 8):
                    pieces.append(pltpu.roll(top, 8 * piece, 1))
                table_high, table_low = split(jnp.concatenate(pieces, axis=0))
                place = slice(block * LANES + inner * z_size, block * LANES + (inner + 1) * z_size)
                high_ref[shift_x, place, :LANES] = table_high
                low_ref[shift_x, place, :LANES] = table_low
                if pair:
                    high_ref[shift_x + 1, place, LANES:] = table_high
                    low_ref[shift_x + 1, place, LANES:] = table_low
        return carry

    lax.fori_loop(0, KERNEL, step, 0)


def pack_taps(padded, z_size, rows):
    packed = LANES // z_size
    group = lax.broadcasted_iota(jnp.int32, (1, 1, LANES), 2) // z_size
    blocks = []
    for block in range(-(-KERNEL // packed)):
        value = padded[:, block * packed : block * packed + rows, :]
        for inner in range(1, packed):
            first = block * packed + inner
            if first < KERNEL:
                value = jnp.where(group == inner, padded[:, first : first + rows, :], value)
        blocks.append(value)
    return blocks


def potential_kernel(sizes, *refs):
    kernels = refs[:3]
    sources = refs[3:7]
    out_ref, whole_ref = refs[7:9]
    scratch = refs[9:]
    padded_refs, table_refs, joined_refs = scratch[:3], scratch[3:9], scratch[9:15]
    arrived = scratch[15 : 15 + len(PLANS)]
    send_sem, recv_sem = scratch[15 + len(PLANS) :]
    copies = halo_copies(sizes, sources, arrived, send_sem, recv_sem)
    for level in (2, 1, 0):
        for index, plan in enumerate(PLANS):
            if plan[0] == level:
                copies[index].start()
    for level in (2, 1, 0):
        build_tables(kernels[level], table_refs[2 * level], table_refs[2 * level + 1], ZS[level], level == 0)
        padded_refs[level][...] = jnp.zeros_like(padded_refs[level])
        padded_refs[level][HALF : HALF + BX[level] + 1, 8 : 8 + RY[level], :] = sources[level][...]
    if True:
        high_table, low_table = table_refs[:2]
        high_table[0, :, LANES:] = jnp.zeros_like(high_table[0, :, LANES:])
        low_table[0, :, LANES:] = jnp.zeros_like(low_table[0, :, LANES:])
        high_table[KERNEL, :, :LANES] = jnp.zeros_like(high_table[0, :, LANES:])
        low_table[KERNEL, :, :LANES] = jnp.zeros_like(low_table[0, :, LANES:])
    results = []
    for level in (2, 1, 0):
        x_out, rows = BX[level] + 1, RY[level]
        padded = padded_refs[level]
        for index, plan in enumerate(PLANS):
            if plan[0] == level:
                copies[index].wait()
        for index, plan in enumerate(PLANS):
            if plan[0] == level:
                size_x, size_y, at_x, at_y = plan[5], plan[7], plan[8], plan[9]
                xs = slice(HALF + at_x, HALF + at_x + size_x)
                ys = slice(8 + at_y, 8 + at_y + size_y)
                padded[xs, ys, :] = padded[xs, ys, :] + arrived[index][...]
        high_table, low_table = table_refs[2 * level], table_refs[2 * level + 1]
        joined_high, joined_low = joined_refs[2 * level], joined_refs[2 * level + 1]
        copied = LANES // ZS[level]
        whole = padded[:, HALF : HALF + rows + KERNEL - 1 + copied, :]
        if level > 0:
            first = 0 if level == 1 else COARSE_LANE
            lanes = lax.broadcasted_iota(jnp.int32, (1, 1, LANES), 2)
            whole = jnp.where((lanes >= first) & (lanes < first + ZS[level]), whole, 0.0)
            spread_out = whole
            for turn in range(1, copied):
                spread_out = spread_out + pltpu.roll(whole, turn * ZS[level], 2)
            whole = spread_out
        for block, value in enumerate(pack_taps(whole, ZS[level], rows)):
            value_high, value_low = split(value)
            joined_high[:, :, block * LANES : (block + 1) * LANES] = value_high
            joined_low[:, :, block * LANES : (block + 1) * LANES] = value_low
        if level > 0:
            total = jnp.zeros((x_out * rows, LANES), jnp.float32)
            for shift_x in range(KERNEL):
                left_high = joined_high[shift_x : shift_x + x_out].reshape(x_out * rows, -1)
                left_low = joined_low[shift_x : shift_x + x_out].reshape(x_out * rows, -1)
                total = total + matmul(left_high, high_table[shift_x])
                total = total + matmul(left_low, high_table[shift_x])
                total = total + matmul(left_high, low_table[shift_x])
        else:
            pairs = (x_out + 1) // 2
            by_pair = [
                ref.reshape(ref.shape[0] // 2, 2, ref.shape[1], ref.shape[2]) for ref in (joined_high, joined_low)
            ]
            both = jnp.zeros((pairs * rows, 2 * LANES), jnp.float32)
            for shift_x in range(KERNEL + 1):
                left_high, left_low = [
                    ref[shift_x // 2 : shift_x // 2 + pairs, shift_x % 2].reshape(pairs * rows, -1) for ref in by_pair
                ]
                both = both + matmul(left_high, high_table[shift_x])
                both = both + matmul(left_low, high_table[shift_x])
                both = both + matmul(left_high, low_table[shift_x])
            total = 0.0
        if level < 2:
            below = results[-1]
            z_low = rows_iota(LANES, LANES)
            lane = lax.broadcasted_iota(jnp.int32, (LANES, LANES), 1)
            lane = lax.rem(lane, ZS[level])
            z_weight = ring_hat(lane.astype(jnp.float32) * 0.5 - z_low.astype(jnp.float32), float(ZS[level + 1]))
            z_weight = jnp.where(z_low < ZS[level + 1], z_weight, 0.0)
            below = exact(below, z_weight)
            rows_below = RY[level + 1]
            count_below = (BX[level + 1] + 1) * rows_below
            fine_row = rows_iota(x_out * rows, count_below)
            low_row = lax.broadcasted_iota(jnp.int32, (x_out * rows, count_below), 1)
            weight = hat((fine_row // rows).astype(jnp.float32) * 0.5 - (low_row // rows_below).astype(jnp.float32))
            weight = weight * hat(
                lax.rem(fine_row, rows).astype(jnp.float32) * 0.5 - lax.rem(low_row, rows_below).astype(jnp.float32)
            )
            total = total + exact(weight, below)
        results.append(total)
    rows = RY[0]
    for x in range(BX[0] + 1):
        piece = results[-1][x * rows : (x + 1) * rows]
        piece = piece + both[(x // 2) * rows : (x // 2 + 1) * rows, (x % 2) * LANES : (x % 2 + 1) * LANES]
        whole_ref[x] = piece
        if x < BX[0]:
            out_ref[x] = piece[: BY[0]]


def force_kernel(count_ref, cell_ref, frac_ref, charge_ref, potential_ref, forces_ref):
    slots = cell_ref.shape[-1]
    rows = RY[0]
    grid_in = potential_ref[...].reshape((BX[0] + 1) * rows, LANES)
    left = jnp.concatenate(split(grid_in), axis=1)
    for start in range(0, slots, CHUNK):
        part = slice(start, start + CHUNK)
        base_x, base_y, base_z = bases(cell_ref[0, :, part])
        frac = [frac_ref[k, 0, :, part] for k in range(3)]
        slot = start + lax.broadcasted_iota(jnp.int32, (1, CHUNK), 1)
        charge = jnp.where(slot < count_ref[0, 0], charge_ref[0, :, part], 0.0)
        row_z = rows_iota(NZ, CHUNK)
        pick_low = jnp.where(row_z == base_z, 1.0, 0.0).astype(jnp.bfloat16)
        pick_high = jnp.where(row_z == lax.rem(base_z + 1, NZ), 1.0, 0.0).astype(jnp.bfloat16)
        low = matmul(left, jnp.concatenate([pick_low, pick_low], axis=0))
        high = matmul(left, jnp.concatenate([pick_high, pick_high], axis=0))
        slope = high - low
        level = low + frac[2] * slope
        row_x = rows_iota(-(-(BX[0] + 1) // 8) * 8, CHUNK)
        row_y = rows_iota(rows, CHUNK)

        def sides(row, base, f):
            lower, upper = row == base, row == base + 1
            weight = jnp.where(lower, 1.0 - f, jnp.where(upper, f, 0.0))
            sign = jnp.where(lower, -1.0, jnp.where(upper, 1.0, 0.0))
            return weight, sign

        weight_x, sign_x = sides(row_x, base_x, frac[0])
        weight_y, sign_y = sides(row_y, base_y, frac[1])
        in_x = jnp.zeros((rows, CHUNK), jnp.float32)
        across_x = jnp.zeros((rows, CHUNK), jnp.float32)
        in_z = jnp.zeros((rows, CHUNK), jnp.float32)
        for x in range(BX[0] + 1):
            piece = level[x * rows : (x + 1) * rows]
            in_x = in_x + weight_x[x : x + 1] * piece
            across_x = across_x + sign_x[x : x + 1] * piece
            in_z = in_z + weight_x[x : x + 1] * slope[x * rows : (x + 1) * rows]
        forces_ref[0, 0, :, part] = -charge * jnp.sum(weight_y * across_x, axis=0, keepdims=True)
        forces_ref[1, 0, :, part] = -charge * jnp.sum(sign_y * in_x, axis=0, keepdims=True)
        forces_ref[2, 0, :, part] = -charge * jnp.sum(weight_y * in_z, axis=0, keepdims=True)


VMEM = pl.BlockSpec(memory_space=pltpu.VMEM)
SMEM = pl.BlockSpec(memory_space=pltpu.SMEM)


def grid_shape(level):
    return jax.ShapeDtypeStruct((BX[level] + 1, RY[level], LANES), jnp.float32)


def solution(mesh):
    sizes = (mesh.shape["gx"], mesh.shape["gy"])

    def per_device(atom_cell, atom_frac, atom_charge, atom_count, fine_kernel, middle_kernel, coarse_kernel):
        slots = atom_cell.shape[-1]
        raw = pl.pallas_call(
            spread_kernel,
            out_shape=(
                grid_shape(0),
                jax.ShapeDtypeStruct((BX[0] + 1, 8, LANES), jnp.float32),
                grid_shape(1),
                grid_shape(2),
            ),
            in_specs=[SMEM, VMEM, VMEM, VMEM],
            out_specs=(VMEM,) * 4,
            name="spread",
        )(atom_count, atom_cell, atom_frac, atom_charge)
        fine, strip, middle, coarse = raw
        padded_shapes, table_shapes, joined_shapes = [], [], []
        for level in range(3):
            packed = LANES // ZS[level]
            depth = -(-KERNEL // packed) * LANES
            x_in = BX[level] + KERNEL + (level == 0)
            width = 2 * LANES if level == 0 else LANES
            padded_shapes.append(pltpu.VMEM((x_in, RY[level] + 24, LANES), jnp.float32))
            table_shapes += [pltpu.VMEM((KERNEL + (level == 0), depth, width), jnp.bfloat16)] * 2
            joined_shapes += [pltpu.VMEM((x_in, RY[level], depth), jnp.bfloat16)] * 2
        landing = [pltpu.VMEM((plan[5], plan[7], LANES), jnp.float32) for plan in PLANS]
        potential, extended = pl.pallas_call(
            lambda *refs: potential_kernel(sizes, *refs),
            out_shape=(jax.ShapeDtypeStruct((CX, CY, NZ), jnp.float32), grid_shape(0)),
            in_specs=[SMEM] * 3 + [VMEM] * 4,
            out_specs=(VMEM, VMEM),
            scratch_shapes=padded_shapes + table_shapes + joined_shapes + landing + [pltpu.SemaphoreType.DMA((len(PLANS),))] * 2,
            compiler_params=pltpu.CompilerParams(collective_id=0, has_side_effects=True),
            name="potential",
        )(fine_kernel, middle_kernel, coarse_kernel, fine, middle, coarse, strip)
        forces = pl.pallas_call(
            force_kernel,
            out_shape=jax.ShapeDtypeStruct((3, 1, 1, slots), jnp.float32),
            in_specs=[SMEM, VMEM, VMEM, VMEM, VMEM],
            out_specs=VMEM,
            name="forces",
        )(atom_count, atom_cell, atom_frac, atom_charge, extended)
        return potential, forces

    return jax.shard_map(
        per_device,
        mesh=mesh,
        in_specs=(
            P("gx", "gy", None),
            P(None, "gx", "gy", None),
            P("gx", "gy", None),
            P("gx", "gy"),
            P(),
            P(),
            P(),
        ),
        out_specs=(P("gx", "gy", None), P(None, "gx", "gy", None)),
        check_vma=False,
    )
```

```python
import jax
import jax.numpy as jnp
from jax import lax
from jax.experimental import pallas as pl
from jax.experimental.pallas import tpu as pltpu
from jax.sharding import PartitionSpec as P

CX = 16
CY = 24
NZ = 128
KERNEL = 9
HALF = KERNEL // 2
LANES = 128
CHUNK = 512
MESH = pl.DeviceIdType.MESH

BX = (CX, CX // 2, CX // 4)
BY = (CY, CY // 2, CY // 4)
RY = tuple(-(-(size + 1) // 8) * 8 for size in BY)
ZS = (NZ, NZ // 2, NZ // 4)
COARSE_LANE = ZS[1]


def split(value):
    high = value.astype(jnp.bfloat16)
    return high, (value - high.astype(jnp.float32)).astype(jnp.bfloat16)


def matmul(a, b):
    return jnp.dot(a, b, preferred_element_type=jnp.float32)


def matmul_nt(a, b):
    return lax.dot_general(a, b, (((1,), (1,)), ((), ())), preferred_element_type=jnp.float32)


def exact(a, b):
    return jnp.dot(a, b, preferred_element_type=jnp.float32, precision=lax.Precision.HIGHEST)


def hat(distance):
    return jnp.maximum(1.0 - jnp.abs(distance), 0.0)


def ring_hat(distance, period):
    distance = jnp.abs(distance)
    return jnp.maximum(1.0 - jnp.minimum(distance, period - distance), 0.0)


def rows_iota(rows, columns):
    return lax.broadcasted_iota(jnp.int32, (rows, columns), 0)


def bases(cell):
    return cell // (CY * NZ), (cell // NZ) % CY, cell % NZ


def spread_kernel(count_ref, cell_ref, frac_ref, charge_ref, fine_ref, strip_ref, middle_ref, upper_ref, coarse_ref):
    slots = cell_ref.shape[-1]
    fine = jnp.zeros((fine_ref.shape[0] * RY[0], LANES), jnp.float32)
    rest = jnp.zeros(((BX[1] + 1) * RY[1] + (BX[2] + 1) * RY[2], LANES), jnp.float32)
    for start in range(0, slots, CHUNK):
        part = slice(start, start + CHUNK)
        base = bases(cell_ref[0, :, part])
        place = [base[k].astype(jnp.float32) + frac_ref[k, 0, :, part] for k in range(3)]
        slot = start + lax.broadcasted_iota(jnp.int32, (1, CHUNK), 1)
        charge = jnp.where(slot < count_ref[0, 0], charge_ref[0, :, part], 0.0)
        tops = []
        for level in range(3):
            scale = 0.5**level
            row_x = rows_iota(-(-(BX[level] + 1) // 8) * 8, CHUNK).astype(jnp.float32)
            row_y = rows_iota(RY[level], CHUNK).astype(jnp.float32)
            weight_x = hat(place[0] * scale - row_x) * charge
            weight_y = hat(place[1] * scale - row_y)
            tops.append(
                jnp.concatenate([weight_x[x : x + 1] * weight_y for x in range(BX[level] + 1)], axis=0)
            )
        z_fine = ring_hat(place[2] - rows_iota(NZ, CHUNK).astype(jnp.float32), float(NZ))
        z_middle = ring_hat(place[2] * 0.5 - rows_iota(ZS[1], CHUNK).astype(jnp.float32), float(ZS[1]))
        z_coarse = ring_hat(place[2] * 0.25 - rows_iota(ZS[2], CHUNK).astype(jnp.float32), float(ZS[2]))
        z_rest = jnp.concatenate([z_middle, z_coarse, jnp.zeros_like(z_coarse)], axis=0)
        for which, top, z_side in ((0, tops[0], z_fine), (1, jnp.concatenate(tops[1:], axis=0), z_rest)):
            top_high, top_low = split(top)
            z_high, z_low = split(z_side)
            both = matmul_nt(top_high, jnp.concatenate([z_high, z_low], axis=0))
            term = both[:, :LANES] + both[:, LANES:] + matmul_nt(top_low, z_high)
            if which == 0:
                fine = fine + term
            else:
                rest = rest + term
    fine = fine.reshape(BX[0] + 1, RY[0], LANES)
    fine_ref[...] = fine
    strip_ref[...] = fine[:, BY[0] - HALF : BY[0] - HALF + 8, :]
    rows = (BX[1] + 1) * RY[1]
    middle = rest[:rows].reshape(BX[1] + 1, RY[1], LANES)
    coarse = rest[rows:].reshape(BX[2] + 1, RY[2], LANES)
    coarse_ref[...] = coarse
    lane = lax.broadcasted_iota(jnp.int32, (1, 1, LANES), 2)
    twice = jnp.concatenate([coarse, coarse], axis=1)
    x_coarse = BX[2] + 1
    top = BX[1] + 1 - x_coarse
    middle_ref[:top] = middle[:top]
    middle_ref[top:] = jnp.where(lane < COARSE_LANE, middle[top:], twice)
    upper_ref[...] = jnp.where(lane < COARSE_LANE, middle[:x_coarse], twice)
    for x in range(HALF + 1):
        middle_ref[top + x, RY[1] - 1 : RY[1], :] = fine[BX[0] - HALF + x, BY[0] : BY[0] + 1, :]
        upper_ref[x, RY[1] - 1 : RY[1], :] = fine[x, BY[0] : BY[0] + 1, :]


def transfers():
    plans, adds = [], ([], [], [])
    reach = HALF + 1
    for dx in (-2, 2):
        for dy in (-1, 0, 1):
            low = 0 if dx < 0 else BX[2]
            adds[2].append((len(plans), 0, 1, 0, RY[2], low - dx * BX[2], -dy * BY[2]))
            plans.append((dx, dy, 2, low, 1, 0, RY[2]))
    for dx in (-1, 0, 1):
        for dy in (-1, 0, 1):
            if dx == 0 and dy == 0:
                continue
            low, size = {-1: (0, reach), 0: (0, BX[1] + 1), 1: (BX[1] - HALF, reach)}[dx]
            low_y, size_y, used = {-1: (0, 8, reach), 0: (0, RY[1], BY[1] + 1), 1: (BY[1] - HALF, 8, reach)}[dy]
            index = len(plans)
            adds[1].append((index, 0, size, 0, used, low - dx * BX[1], low_y - dy * BY[1]))
            ride = BX[1] - HALF if dx == 0 else 0
            adds[2].append((index, ride, BX[2] + 1, 0, BY[2] + 1, -dx * BX[2], -dy * BY[2]))
            if dx != 0 and dy == 0:
                low_x = 0 if dx < 0 else BX[0] - HALF
                adds[0].append((index, 0, reach, RY[1] - 1, 1, low_x - dx * BX[0], BY[0]))
            plans.append((dx, dy, 4 if dx < 0 else 1, low, size, low_y, size_y))
    for dx in (-1, 0, 1):
        for dy in (-1, 0, 1):
            if dx == 0 and dy == 0:
                continue
            low, size = {-1: (0, reach), 0: (0, BX[0] + 1), 1: (BX[0] - HALF, reach)}[dx]
            source, size_y, first_y = {-1: (0, 8, 0), 0: (0, BY[0], 0), 1: (3, 8, BY[0] - HALF)}[dy]
            used = min(size_y, reach) if dy else size_y
            adds[0].append((len(plans), 0, size, 0, used, low - dx * BX[0], first_y - dy * BY[0]))
            plans.append((dx, dy, source, low, size, 0, size_y))
    return plans, adds


PLANS, ADDS = transfers()


def halo_copies(sizes, sources, targets, send_sem, recv_sem):
    me = (lax.axis_index("gx"), lax.axis_index("gy"))

    def device(dx, dy):
        return (lax.rem(me[0] + dx + sizes[0], sizes[0]), lax.rem(me[1] + dy + sizes[1], sizes[1]))

    barrier = pltpu.get_barrier_semaphore()
    around = sorted({plan[:2] for plan in PLANS})
    for dx, dy in around:
        pl.semaphore_signal(barrier, inc=1, device_id=device(dx, dy), device_id_type=MESH)
    pl.semaphore_wait(barrier, len(around))
    copies = []
    for index, (dx, dy, source, low_x, size_x, low_y, size_y) in enumerate(PLANS):
        copies.append(
            pltpu.make_async_remote_copy(
                src_ref=sources[source].at[pl.ds(low_x, size_x), pl.ds(low_y, size_y)],
                dst_ref=targets[index],
                send_sem=send_sem.at[index],
                recv_sem=recv_sem.at[index],
                device_id=device(dx, dy),
                device_id_type=MESH,
            )
        )
    return copies


def build_tables(kernel_ref, high_ref, low_ref, z_size, pair):
    packed = LANES // z_size
    blocks = -(-KERNEL // packed)
    row = rows_iota(8, LANES)
    lane = lax.broadcasted_iota(jnp.int32, (8, LANES), 1)
    tap = lax.rem(row - lane + HALF + 2 * LANES, z_size)

    def step(shift_x, carry):
        for block in range(blocks):
            for inner in range(packed):
                shift_y = block * packed + inner
                top = jnp.zeros((8, LANES), jnp.float32)
                if shift_y < KERNEL:
                    for c in range(KERNEL):
                        value = kernel_ref[shift_x, shift_y, c]
                        top = jnp.where(tap == c, value, top)
                pieces = [top]
                for piece in range(1, z_size // 8):
                    pieces.append(pltpu.roll(top, 8 * piece, 1))
                table_high, table_low = split(jnp.concatenate(pieces, axis=0))
                place = slice(block * LANES + inner * z_size, block * LANES + (inner + 1) * z_size)
                high_ref[shift_x, place, :LANES] = table_high
                low_ref[shift_x, place, :LANES] = table_low
                if pair:
                    high_ref[shift_x + 1, place, LANES:] = table_high
                    low_ref[shift_x + 1, place, LANES:] = table_low
        return carry

    lax.fori_loop(0, KERNEL, step, 0)


def pack_taps(padded, z_size, rows):
    packed = LANES // z_size
    group = lax.broadcasted_iota(jnp.int32, (1, 1, LANES), 2) // z_size
    blocks = []
    for block in range(-(-KERNEL // packed)):
        value = padded[:, HALF + block * packed : HALF + block * packed + rows, :]
        for inner in range(1, packed):
            first = block * packed + inner
            if first < KERNEL:
                value = jnp.where(group == inner, padded[:, HALF + first : HALF + first + rows, :], value)
        blocks.append(value)
    return blocks


def potential_kernel(sizes, *refs):
    kernels = refs[:3]
    sources = refs[3:8]
    out_ref, whole_ref = refs[8:10]
    scratch = refs[10:]
    padded_refs, table_refs, joined_refs = scratch[:3], scratch[3:9], scratch[9:15]
    arrived = scratch[15 : 15 + len(PLANS)]
    send_sem, recv_sem, raised_ref = scratch[15 + len(PLANS) :]
    copies = halo_copies(sizes, sources, arrived, send_sem, recv_sem)
    for copy in copies:
        copy.start()
    for level in (2, 1, 0):
        build_tables(kernels[level], table_refs[2 * level], table_refs[2 * level + 1], ZS[level], level == 0)
        padded_refs[level][...] = jnp.zeros_like(padded_refs[level])
        used = BY[level] + 1
        padded_refs[level][HALF : HALF + BX[level] + 1, 8 : 8 + used, :] = sources[level][:, :used, :]
    if True:
        high_table, low_table = table_refs[:2]
        high_table[0, :, LANES:] = jnp.zeros_like(high_table[0, :, LANES:])
        low_table[0, :, LANES:] = jnp.zeros_like(low_table[0, :, LANES:])
        high_table[KERNEL, :, :LANES] = jnp.zeros_like(high_table[0, :, LANES:])
        low_table[KERNEL, :, :LANES] = jnp.zeros_like(low_table[0, :, LANES:])
    results = []
    waited = set()
    for level in (2, 1, 0):
        x_out, rows = BX[level] + 1, RY[level]
        padded = padded_refs[level]
        if level < 2:
            below = results[-1]
            z_low = rows_iota(LANES, LANES)
            lane = lax.broadcasted_iota(jnp.int32, (LANES, LANES), 1)
            lane = lax.rem(lane, ZS[level])
            z_weight = ring_hat(lane.astype(jnp.float32) * 0.5 - z_low.astype(jnp.float32), float(ZS[level + 1]))
            z_weight = jnp.where(z_low < ZS[level + 1], z_weight, 0.0)
            below = exact(below, z_weight)
            rows_below = RY[level + 1]
            count_below = (BX[level + 1] + 1) * rows_below
            fine_row = rows_iota(x_out * rows, count_below)
            low_row = lax.broadcasted_iota(jnp.int32, (x_out * rows, count_below), 1)
            weight = hat((fine_row // rows).astype(jnp.float32) * 0.5 - (low_row // rows_below).astype(jnp.float32))
            weight = weight * hat(
                lax.rem(fine_row, rows).astype(jnp.float32) * 0.5 - lax.rem(low_row, rows_below).astype(jnp.float32)
            )
            raised = exact(weight, below)
            if level == 0:
                raised_ref[...] = raised
        for index in sorted({add[0] for add in ADDS[level]}):
            if index not in waited:
                copies[index].wait()
                waited.add(index)
        for index, from_x, size_x, from_y, size_y, at_x, at_y in ADDS[level]:
            xs = slice(HALF + at_x, HALF + at_x + size_x)
            ys = slice(8 + at_y, 8 + at_y + size_y)
            piece = arrived[index][from_x : from_x + size_x, from_y : from_y + size_y, :]
            padded[xs, ys, :] = padded[xs, ys, :] + piece
        high_table, low_table = table_refs[2 * level], table_refs[2 * level + 1]
        joined_high, joined_low = joined_refs[2 * level], joined_refs[2 * level + 1]
        copied = LANES // ZS[level]
        if level > 0:
            whole = padded[...]
            first = 0 if level == 1 else COARSE_LANE
            lanes = lax.broadcasted_iota(jnp.int32, (1, 1, LANES), 2)
            whole = jnp.where((lanes >= first) & (lanes < first + ZS[level]), whole, 0.0)
            spread_out = whole
            for turn in range(1, copied):
                spread_out = spread_out + pltpu.roll(whole, turn * ZS[level], 2)
            padded[...] = spread_out
        for block, value in enumerate(pack_taps(padded, ZS[level], rows)):
            value_high, value_low = split(value)
            joined_high[:, :, block * LANES : (block + 1) * LANES] = value_high
            joined_low[:, :, block * LANES : (block + 1) * LANES] = value_low
        if level > 0:
            total = jnp.zeros((x_out * rows, LANES), jnp.float32)
            for shift_x in range(KERNEL):
                left_high = joined_high[shift_x : shift_x + x_out].reshape(x_out * rows, -1)
                left_low = joined_low[shift_x : shift_x + x_out].reshape(x_out * rows, -1)
                total = total + matmul(left_high, high_table[shift_x])
                total = total + matmul(left_low, high_table[shift_x])
                total = total + matmul(left_high, low_table[shift_x])
        else:
            pairs = (x_out + 1) // 2
            by_pair = [
                ref.reshape(ref.shape[0] // 2, 2, ref.shape[1], ref.shape[2]) for ref in (joined_high, joined_low)
            ]
            both = jnp.zeros((pairs * rows, 2 * LANES), jnp.float32)
            for shift_x in range(KERNEL + 1):
                left_high, left_low = [
                    ref[shift_x // 2 : shift_x // 2 + pairs, shift_x % 2].reshape(pairs * rows, -1) for ref in by_pair
                ]
                both = both + matmul(left_high, high_table[shift_x])
                both = both + matmul(left_low, high_table[shift_x])
                both = both + matmul(left_high, low_table[shift_x])
            total = None
        if level == 1:
            total = total + raised
        results.append(total)
    rows = RY[0]
    for x in range(BX[0] + 1):
        piece = raised_ref[x * rows : (x + 1) * rows]
        piece = piece + both[(x // 2) * rows : (x // 2 + 1) * rows, (x % 2) * LANES : (x % 2 + 1) * LANES]
        whole_ref[x] = piece
        if x < BX[0]:
            out_ref[x] = piece[: BY[0]]


def force_kernel(count_ref, cell_ref, frac_ref, charge_ref, potential_ref, forces_ref):
    slots = cell_ref.shape[-1]
    rows = RY[0]
    grid_in = potential_ref[...].reshape((BX[0] + 1) * rows, LANES)
    left = jnp.concatenate(split(grid_in), axis=1)
    for start in range(0, slots, CHUNK):
        part = slice(start, start + CHUNK)
        base_x, base_y, base_z = bases(cell_ref[0, :, part])
        frac = [frac_ref[k, 0, :, part] for k in range(3)]
        slot = start + lax.broadcasted_iota(jnp.int32, (1, CHUNK), 1)
        charge = jnp.where(slot < count_ref[0, 0], charge_ref[0, :, part], 0.0)
        row_z = rows_iota(NZ, CHUNK)
        pick_low = jnp.where(row_z == base_z, 1.0, 0.0).astype(jnp.bfloat16)
        pick_high = jnp.where(row_z == lax.rem(base_z + 1, NZ), 1.0, 0.0).astype(jnp.bfloat16)
        low = matmul(left, jnp.concatenate([pick_low, pick_low], axis=0))
        high = matmul(left, jnp.concatenate([pick_high, pick_high], axis=0))
        slope = high - low
        level = low + frac[2] * slope
        row_x = rows_iota(-(-(BX[0] + 1) // 8) * 8, CHUNK)
        row_y = rows_iota(rows, CHUNK)

        def sides(row, base, f):
            lower, upper = row == base, row == base + 1
            weight = jnp.where(lower, 1.0 - f, jnp.where(upper, f, 0.0))
            sign = jnp.where(lower, -1.0, jnp.where(upper, 1.0, 0.0))
            return weight, sign

        weight_x, sign_x = sides(row_x, base_x, frac[0])
        weight_y, sign_y = sides(row_y, base_y, frac[1])
        in_x = jnp.zeros((rows, CHUNK), jnp.float32)
        across_x = jnp.zeros((rows, CHUNK), jnp.float32)
        in_z = jnp.zeros((rows, CHUNK), jnp.float32)
        for x in range(BX[0] + 1):
            piece = level[x * rows : (x + 1) * rows]
            in_x = in_x + weight_x[x : x + 1] * piece
            across_x = across_x + sign_x[x : x + 1] * piece
            in_z = in_z + weight_x[x : x + 1] * slope[x * rows : (x + 1) * rows]
        forces_ref[0, 0, :, part] = -charge * jnp.sum(weight_y * across_x, axis=0, keepdims=True)
        forces_ref[1, 0, :, part] = -charge * jnp.sum(sign_y * in_x, axis=0, keepdims=True)
        forces_ref[2, 0, :, part] = -charge * jnp.sum(weight_y * in_z, axis=0, keepdims=True)


VMEM = pl.BlockSpec(memory_space=pltpu.VMEM)
SMEM = pl.BlockSpec(memory_space=pltpu.SMEM)


def grid_shape(level):
    return jax.ShapeDtypeStruct((BX[level] + 1, RY[level], LANES), jnp.float32)


def solution(mesh):
    sizes = (mesh.shape["gx"], mesh.shape["gy"])

    def per_device(atom_cell, atom_frac, atom_charge, atom_count, fine_kernel, middle_kernel, coarse_kernel):
        slots = atom_cell.shape[-1]
        raw = pl.pallas_call(
            spread_kernel,
            out_shape=(
                grid_shape(0),
                jax.ShapeDtypeStruct((BX[0] + 1, 8, LANES), jnp.float32),
                grid_shape(1),
                jax.ShapeDtypeStruct((BX[2] + 1, RY[1], LANES), jnp.float32),
                grid_shape(2),
            ),
            in_specs=[SMEM, VMEM, VMEM, VMEM],
            out_specs=(VMEM,) * 5,
            name="spread",
        )(atom_count, atom_cell, atom_frac, atom_charge)
        fine, strip, middle, upper, coarse = raw
        padded_shapes, table_shapes, joined_shapes = [], [], []
        for level in range(3):
            packed = LANES // ZS[level]
            depth = -(-KERNEL // packed) * LANES
            x_in = BX[level] + KERNEL + (level == 0)
            width = 2 * LANES if level == 0 else LANES
            padded_shapes.append(pltpu.VMEM((x_in, RY[level] + 24, LANES), jnp.float32))
            table_shapes += [pltpu.VMEM((KERNEL + (level == 0), depth, width), jnp.bfloat16)] * 2
            joined_shapes += [pltpu.VMEM((x_in, RY[level], depth), jnp.bfloat16)] * 2
        landing = [pltpu.VMEM((plan[4], plan[6], LANES), jnp.float32) for plan in PLANS]
        potential, extended = pl.pallas_call(
            lambda *refs: potential_kernel(sizes, *refs),
            out_shape=(jax.ShapeDtypeStruct((CX, CY, NZ), jnp.float32), grid_shape(0)),
            in_specs=[SMEM] * 3 + [VMEM] * 5,
            out_specs=(VMEM, VMEM),
            scratch_shapes=padded_shapes
            + table_shapes
            + joined_shapes
            + landing
            + [pltpu.SemaphoreType.DMA((len(PLANS),))] * 2
            + [pltpu.VMEM(((BX[0] + 1) * RY[0], LANES), jnp.float32)],
            compiler_params=pltpu.CompilerParams(collective_id=0, has_side_effects=True),
            name="potential",
        )(fine_kernel, middle_kernel, coarse_kernel, fine, middle, coarse, strip, upper)
        forces = pl.pallas_call(
            force_kernel,
            out_shape=jax.ShapeDtypeStruct((3, 1, 1, slots), jnp.float32),
            in_specs=[SMEM, VMEM, VMEM, VMEM, VMEM],
            out_specs=VMEM,
            name="forces",
        )(atom_count, atom_cell, atom_frac, atom_charge, extended)
        return potential, forces

    return jax.shard_map(
        per_device,
        mesh=mesh,
        in_specs=(
            P("gx", "gy", None),
            P(None, "gx", "gy", None),
            P("gx", "gy", None),
            P("gx", "gy"),
            P(),
            P(),
            P(),
        ),
        out_specs=(P("gx", "gy", None), P(None, "gx", "gy", None)),
        check_vma=False,
    )
```
